32 devices in a mesh: row: 4 (over y, x), col: 8 (over z, core).
Axes of the slice: x: 2, y: 2, z: 4, core: 2. Of those that a mesh axis runs over, the one named last changes fastest.
Arguments:
- queries: float32 [2, 192, 20480], P(None, 'col', 'row'), may hold values from -6 to 6
- precond: float32 [20480, 20480], P('row', 'col'), may hold values from -0.0390625 to 0.0390625
- column_gain: float32 [20480], P('col'), may hold values from 0.5 to 2
- store: bfloat16 [12288, 20480], P('row', 'col'), may hold values from -0.0390625 to 0.0390625
Outputs:
- scores: float32 [2, 192, 12288], P(None, 'col', 'row')
The draws below stay inside these ranges and needn't reach their ends.
All inputs are finite; a program needn't handle non-finite values.
Results may differ from the reference program's by a relative error of at most 0.0029.
Values sent between devices are 32-bit elements; how exact they have to be, the bound alone decides.
No kernel may reach another device: no remote copies, remote signals or barrier semaphores. Data moves between devices by JAX's collectives and lax.ppermute only.
A program may use at most 128 MiB of HBM per device.

```python
import math
import jax
import jax.numpy as jnp
from jax import lax

G = 20480
BATCHES = 2
QB = 192
DOCS = 12288


def block_levels(own_key, extent, cuts, least, top_value):
    level, own = 1.0, jax.random.fold_in(own_key, 6)
    for axis_at, parts in cuts:
        steps = jnp.exp(jax.random.uniform(jax.random.fold_in(own, axis_at), (parts,), jnp.float32, least / len(cuts), top_value / len(cuts)))
        level = level * jnp.repeat(steps, extent[axis_at] // parts).reshape([-1 if axis == axis_at else 1 for axis in range(len(extent))])
    return level


def gaussian(own_key, dims, width, reach, pieces=(), held_as=jnp.bfloat16):
    array = width * jax.random.normal(own_key, dims, jnp.float32)
    if pieces:
        array = array * block_levels(own_key, dims, pieces, -0.22, 0.18)
    return jnp.clip(array, -reach, reach).astype(held_as)


def setup_inputs(seed: int = 0) -> dict:
    seeds = jax.random.split(jax.random.key(seed), 5)
    return {
        "queries": gaussian(seeds[0], (BATCHES, QB, G), 1.0, 6.0, ((1, 8), (2, 4)), jnp.float32),
        "precond": gaussian(seeds[1], (G, G), G ** -0.5, 0.0390625, ((0, 4), (1, 8)), jnp.float32),
        "column_gain": jnp.clip(jnp.exp(math.log(2.0) - 1.3862944 * jax.random.uniform(seeds[2], (G,), jnp.float32) ** block_levels(seeds[2], (G,), ((0, 8),), -0.2, 0.2)), 0.5, 2.0),
        "store": gaussian(seeds[3], (DOCS, G), G ** -0.5, 0.0390625, ((0, 4), (1, 8))),
    }


def reference(queries, precond, column_gain, store):
    results = []
    for batch_index in range(BATCHES):
        conditioned = jnp.dot(queries[batch_index], precond, precision=lax.Precision.HIGHEST, preferred_element_type=jnp.float32)
        lowered = (conditioned * column_gain[None, :]).astype(jnp.bfloat16)
        results.append(jnp.dot(lowered, store.T, preferred_element_type=jnp.float32))
    return jnp.stack(results)
```

```python
import functools

import jax
import jax.numpy as jnp
from jax import lax
from jax.experimental import pallas as pl
from jax.experimental.pallas import tpu as pltpu
from jax.sharding import PartitionSpec as P


MIB = 1024 * 1024
WHOLE = pl.BlockSpec(memory_space=pltpu.VMEM)
ALL = ("row", "col")


def split(x):
    high = x.astype(jnp.bfloat16)
    return high, (x - high.astype(jnp.float32)).astype(jnp.bfloat16)


def fitting(extent, most):
    sizes = [s for s in range(128, most + 1, 128) if extent % s == 0]
    return max(sizes) if sizes else extent


def condition_kernel(parts, priors, me_ref, *refs):
    x_refs, prior_refs, p_ref = refs[:parts], refs[parts : parts + priors], refs[parts + priors]
    out_refs, (lhs, total) = refs[parts + priors + 1 : -2], refs[-2:]
    height, tile = total.shape
    rows = height // len(out_refs)

    @pl.when(pl.program_id(0) == 0)
    def _():
        at = 0
        for x_ref in x_refs:
            n = x_ref.shape[0]
            high, low = split(x_ref[...])
            lhs[at : at + n, :] = high
            lhs[height + at : height + at + n, :] = low
            at += n

    p_high, p_low = split(p_ref[...])
    both = jnp.dot(lhs[...], p_high, preferred_element_type=jnp.float32)
    cross = jnp.dot(lhs[:height, :], p_low, preferred_element_type=jnp.float32)
    total[...] = both[:height] + (both[height:] + cross)
    columns = pl.ds(pl.multiple_of(pl.program_id(0) * tile, 128), tile)
    if len(out_refs) == 1:
        out_refs[0][:, columns] = total[...]
        return
    for slot, out_ref in enumerate(out_refs):
        group = pl.ds(pl.multiple_of((me_ref[0] ^ slot) * rows, 8), rows)
        for n, prior_ref in enumerate(prior_refs):
            out_ref[n * rows : (n + 1) * rows, columns] = prior_ref[group, columns]
        out_ref[priors * rows :, columns] = total[group, :]


def condition(me, xs, priors, precond, owners):
    height, (depth, width) = sum(x.shape[0] for x in xs), precond.shape
    rows = (1 + len(priors)) * height // owners
    tile = fitting(width, 256)
    return pl.pallas_call(
        functools.partial(condition_kernel, len(xs), len(priors)),
        out_shape=[jax.ShapeDtypeStruct((rows, width), jnp.float32)] * owners,
        grid_spec=pltpu.PrefetchScalarGridSpec(
            num_scalar_prefetch=1,
            grid=(width // tile,),
            in_specs=[WHOLE] * (len(xs) + len(priors))
            + [pl.BlockSpec((depth, tile), lambda j, me: (0, j))],
            out_specs=[WHOLE] * owners,
            scratch_shapes=[
                pltpu.VMEM((2 * height, depth), jnp.bfloat16),
                pltpu.VMEM((height, tile), jnp.float32),
            ],
        ),
        compiler_params=pltpu.CompilerParams(vmem_limit_bytes=24 * MIB),
        cost_estimate=pl.CostEstimate(
            flops=6 * height * depth * width, transcendentals=0, bytes_accessed=4 * depth * width
        ),
        name="condition",
    )(me, *xs, *priors, precond)


def score_kernel(owners, count, me_ref, *refs):
    y_refs, gain_ref, s_ref = refs[:owners], refs[owners], refs[owners + 1]
    keep_ref, send_ref, wide, lhs = refs[-4:]
    half = keep_ref.shape[0]
    height = half * 2 // count
    rows = height // owners

    @pl.when(pl.program_id(0) == 0)
    def _():
        for n in range(count):
            for slot, y_ref in enumerate(y_refs):
                group = pl.ds(pl.multiple_of((me_ref[0] ^ slot) * rows, 8), rows)
                wide[group, :] = y_ref[n * rows : (n + 1) * rows, :] * gain_ref[...]
            at = n * height // 2
            lhs[at : at + height // 2, :] = wide[: height // 2, :].astype(jnp.bfloat16)
            lhs[half + at : half + at + height // 2, :] = wide[height // 2 :, :].astype(jnp.bfloat16)

    tile = fitting(keep_ref.shape[1], 1024)
    columns = pl.ds(pl.multiple_of(pl.program_id(0) * tile, 128), tile)
    product = lax.dot_general(
        lhs[...], s_ref[columns, :], (((1,), (1,)), ((), ())), preferred_element_type=jnp.float32
    )
    keep_ref[:, columns] = product[:half]
    send_ref[:, columns] = product[half:]


def score(me, ys, count, gain, store):
    docs, depth = store.shape
    height = sum(y.shape[0] for y in ys)
    tile = fitting(docs, 1024)
    return pl.pallas_call(
        functools.partial(score_kernel, len(ys), count),
        out_shape=[jax.ShapeDtypeStruct((height // 2, docs), jnp.float32)] * 2,
        grid_spec=pltpu.PrefetchScalarGridSpec(
            num_scalar_prefetch=1,
            grid=(docs // tile,),
            in_specs=[WHOLE] * (len(ys) + 2),
            out_specs=[WHOLE] * 2,
            scratch_shapes=[
                pltpu.VMEM((height // count, depth), jnp.float32),
                pltpu.VMEM((height, depth), jnp.bfloat16),
            ],
        ),
        compiler_params=pltpu.CompilerParams(vmem_limit_bytes=12 * MIB),
        cost_estimate=pl.CostEstimate(
            flops=2 * height * depth * docs, transcendentals=0, bytes_accessed=2 * docs * depth
        ),
        name="score",
    )(me, *ys, gain, store)


def local(row_size, col_size, queries, precond, column_gain, store):
    line = col_size // 2
    me = lax.axis_index("row").astype(jnp.int32).reshape(1)

    def send(x, target):
        pairs = []
        for r in range(row_size):
            for c in range(col_size):
                to = target(r, c // 2, c % 2)
                if to is not None:
                    pairs.append((r * col_size + c, to[0] * col_size + to[1] * 2 + to[2]))
        return lax.ppermute(x, ALL, pairs)

    def to_row(x, s):
        return send(x, lambda r, z, k: (r ^ s, z, k))

    def to_line(x, s):
        return send(x, lambda r, z, k: (r, z ^ s, k))

    def swap(x):
        return send(x, lambda r, z, k: (r, z, 1 - k))

    batches, own_rows, depth = queries.shape
    own = queries.reshape(batches * own_rows, depth)
    unit = batches * own_rows

    if line == 4:
        middle = lambda r, z, k: (r, 3 - z, k) if z in (1, 2) else None
        outward = lambda r, z, k: (r, 0 if z == 1 else 3, k) if z in (1, 2) else None
        near = to_line(own, 1)
        mid_own = send(own, middle)
        mid_near = send(near, middle)
        slots = [own, near, mid_near + send(mid_own, outward), mid_own + send(mid_near, outward)]
    else:
        slots = [own] + [to_line(own, s) for s in range(1, line)]

    pair = 1 if (2 * unit) % (8 * row_size) == 0 else 2
    firsts = list(range(0, line, pair))
    batches_of = [firsts[:2]] + [[first] for first in firsts[2:]] if pair == 1 else [[f] for f in firsts]
    gain = column_gain[None, :]
    kept = {}
    scored = []
    for batch in batches_of:
        priors = []
        for first in batch:
            group = slots[first : first + pair]
            xs = group + [swap(x) for x in group]
            last = first == batch[-1]
            outs = condition(me, xs, priors if last else [], precond, row_size if last else 1)
            if not last:
                priors = priors + list(outs)
        mine = outs[0]
        for s, other in enumerate(outs[1:]):
            mine = mine + to_row(other, s + 1)
        scored.append((batch, [mine] + [to_row(mine, s) for s in range(1, row_size)]))

    for batch, ys in scored:
        keep, away = score(me, ys, len(batch), gain, store)
        back = swap(away)
        done = [first + n for first in batch for n in range(pair)]
        for n, slot in enumerate(done):
            rows = slice(n * unit, (n + 1) * unit)
            kept[slot] = keep[rows] + back[rows]
    result = kept[0]
    for s in range(1, line):
        result = result + to_line(kept[s], s)
    return result.reshape(batches, own_rows, store.shape[0])


def solution(mesh):
    row_size, col_size = mesh.shape["row"], mesh.shape["col"]

    def body(*arrays):
        return local(row_size, col_size, *arrays)

    return jax.shard_map(
        body,
        mesh=mesh,
        in_specs=(P(None, "col", "row"), P("row", "col"), P("col"), P("row", "col")),
        out_specs=P(None, "col", "row"),
        check_vma=False,
    )
```
